32 devices in a mesh: group: 2 (over x), fsdp: 16 (over z, y, core).
Axes of the slice: x: 2, y: 2, z: 4, core: 2. Of those that a mesh axis runs over, the one named last changes fastest.
Arguments:
- tokens: bfloat16 [4096, 4096], P(('group', 'fsdp')), parts along dimension 0, may hold values from -6 to 6
- gate_cot: bfloat16 [4096, 16384], P(('group', 'fsdp')), parts along dimension 0, may hold values from -6 to 6
- gate_weight: bfloat16 [4096, 16384], P(None, 'fsdp'), may hold values from -0.15625 to 0.15625
- keep_mask: int32 [32, 128], P(None, 'fsdp'), may hold values from 0 to 1, as said below
Outputs:
- gate_out: bfloat16 [4096, 16384], P(('group', 'fsdp')), parts along dimension 0
- grad_tiles: bfloat16 [256, 12, 128, 128], P(('group', 'fsdp')), parts along dimension 0
The draws below stay inside these ranges and needn't reach their ends.
There are 2 independent parts, one for each index of `group`. The reference program is written for one: setup_inputs(seed, part) draws one part's arguments, and reference() takes and returns one part's arrays. A program takes and returns all parts, laid end to end along the dimension named above; an argument that names none is the same for every part. Nothing has to cross between parts.
Inputs may be any that keep to these rules, and one draw needn't show every extreme that they name: `keep_mask`: each tile column keeps between 8 and 12 tiles; some column keeps exactly 12.
All inputs are finite; a program needn't handle non-finite values.
Results may differ from the reference program's by a relative error of at most 0.001.
Values may be sent and summed in bfloat16 or wider, within the bound.
A program may use at most 256 MiB of HBM per device.

```python
import jax
import jax.numpy as jnp

D = 4096
FW = 16384
TILE = 128
RT = 32
CT = 128
KMAX = 12
TOKENS = 2048


def draw_keep_mask(key, part):
    base = jax.random.fold_in(key, 11)
    key_count, key_pick, key_order = jax.random.split(base, 3)
    kept_count = jax.random.randint(key_count, (CT,), RT // 4, KMAX + 1)
    chosen = jax.random.randint(key_pick, (), 0, CT)
    kept_count = jnp.where(jnp.arange(CT) == chosen, KMAX, kept_count)
    scores = jax.random.randint(key_order, (RT, CT), 0, 1 << 20) * RT + jnp.arange(RT)[:, None]
    ranking = jnp.argsort(jnp.argsort(scores, axis=0), axis=0)
    return (ranking < kept_count[None, :]).astype(jnp.int32)


def shard_levels(own_key, extent, shards, least, largest):
    loudness = 1.0
    for axis_at, parts in shards:
        steps = jax.random.uniform(jax.random.fold_in(jax.random.fold_in(own_key, 6), axis_at), (parts,), jnp.float32, least / len(shards), largest / len(shards))
        loudness = loudness * jnp.repeat(jnp.exp(steps), extent[axis_at] // parts).reshape((-1,) + (1,) * (len(extent) - 1 - axis_at))
    return loudness


def normal_values(key, shape, spread, bound, pieces=(), held_as=jnp.bfloat16):
    array = jax.random.normal(key, shape, jnp.float32) * spread
    if len(pieces) > 0:
        array = shard_levels(key, shape, pieces, -0.22, 0.18) * array
    return jnp.clip(array, min=-bound, max=bound).astype(held_as)


def setup_inputs(seed: int = 0, part: int = 0) -> dict:
    arg_keys = jax.random.split(jax.random.key(seed), 5)
    part_splits = jax.random.split(jax.random.fold_in(arg_keys[4], part), 5)
    tokens = normal_values(part_splits[0], (TOKENS, D), 1.0, 6.0, ((0, 16),))
    gate_cot = normal_values(part_splits[1], (TOKENS, FW), 1.0, 6.0, ((0, 16),))
    gate_weight = normal_values(arg_keys[2], (D, FW), (KMAX * TILE) ** -0.5, 0.15625, ((1, 16),))
    keep_mask = draw_keep_mask(jax.random.fold_in(arg_keys[4], 71), part)
    return {"tokens": tokens, "gate_cot": gate_cot, "gate_weight": gate_weight, "keep_mask": keep_mask}


def reference(tokens, gate_cot, gate_weight, keep_mask):
    tile_mask = jnp.repeat(jnp.repeat(keep_mask, TILE, axis=0), TILE, axis=1)
    pruned = jnp.where(tile_mask > 0, gate_weight, jnp.zeros_like(gate_weight))
    gate_out = jnp.dot(tokens, pruned, preferred_element_type=jnp.float32).astype(jnp.bfloat16)
    full = jnp.dot(tokens.T, gate_cot, preferred_element_type=jnp.float32)
    tiles = full.reshape(RT, TILE, CT, TILE).transpose(2, 0, 1, 3)
    kept_count = jnp.sum(keep_mask, axis=0)
    ordering = jnp.argsort(1 - keep_mask, axis=0, stable=True)[:KMAX].T.astype(jnp.int32)
    picked = jnp.take_along_axis(tiles, ordering[:, :, None, None], axis=1)
    valid = jnp.arange(KMAX)[None, :] < kept_count[:, None]
    picked = jnp.where(valid[:, :, None, None], picked, jnp.zeros_like(picked))
    return gate_out, picked.astype(jnp.bfloat16)
```

```python
import jax
import jax.numpy as jnp
from jax import lax
from jax.experimental import pallas as pl
from jax.experimental.pallas import tpu as pltpu
from jax.sharding import PartitionSpec as P

TILE = 128
RT = 32
KMAX = 12


def kept_lists(keep_mask):
    kept_count = jnp.sum(keep_mask, axis=0)
    ordering = jnp.argsort(1 - keep_mask, axis=0, stable=True)[:KMAX]
    kept_rows = ordering.T
    kept_valid = jnp.arange(KMAX)[None, :] < kept_count[:, None]
    return (kept_rows, kept_valid)


def column_tiles(gate_weight, kept_rows, kept_valid, column):
    strip = gate_weight[:, column * TILE : (column + 1) * TILE].reshape(RT, TILE, TILE)
    picked = jnp.stack(
        [lax.dynamic_index_in_dim(strip, kept_rows[column, k], 0, False) for k in range(KMAX)]
    )
    picked = jnp.where(kept_valid[column][:, None, None], picked, jnp.zeros_like(picked))
    return picked.reshape(KMAX * TILE, TILE)


def general_path(tokens, gate_cot, gate_weight, keep_mask):
    local_width = gate_weight.shape[1]
    local_cols = local_width // TILE
    kept_rows, kept_valid = kept_lists(keep_mask)
    weight_cols = [
        column_tiles(gate_weight, kept_rows, kept_valid, column) for column in range(local_cols)
    ]
    cot_cols = lax.all_to_all(gate_cot, "fsdp", split_axis=1, concat_axis=0, tiled=True)
    total_rows = cot_cols.shape[0]

    def block_work(carry, piece, start):
        gate_all, grads = carry
        length = piece.shape[0]
        slope_piece = lax.dynamic_slice_in_dim(cot_cols, start, length, 0)
        outputs = []
        new_grads = []
        for column in range(local_cols):
            selected = jnp.concatenate(
                [
                    lax.dynamic_slice_in_dim(piece, kept_rows[column, k] * TILE, TILE, 1)
                    for k in range(KMAX)
                ],
                axis=1,
            )
            outputs.append(
                jnp.dot(selected, weight_cols[column], preferred_element_type=jnp.float32)
            )
            slope_col = slope_piece[:, column * TILE : (column + 1) * TILE]
            grad_col = lax.dot_general(
                selected, slope_col, (((0,), (0,)), ((), ())), preferred_element_type=jnp.float32
            )
            new_grads.append(grad_col.reshape(KMAX, TILE, TILE))
        values = jnp.concatenate(outputs, axis=1).astype(jnp.bfloat16)
        gate_all = lax.dynamic_update_slice_in_dim(gate_all, values, start, 0)
        return (gate_all, grads + jnp.stack(new_grads, axis=0))

    initial = (
        jnp.zeros((total_rows, local_width), jnp.bfloat16),
        jnp.zeros((local_cols, KMAX, TILE, TILE), jnp.float32),
    )
    piece = lax.all_gather(tokens, "fsdp", axis=0, tiled=True)
    length = piece.shape[0]

    def one_block(index, inner):
        offset = index * 1024
        block_rows = lax.dynamic_slice_in_dim(piece, offset, 1024, 0)
        return block_work(inner, block_rows, offset)

    gate_cols, partial_tiles = lax.fori_loop(0, length // 1024, one_block, initial)
    gate_out = lax.all_to_all(gate_cols, "fsdp", split_axis=0, concat_axis=1, tiled=True)
    grad_tiles = jnp.where(
        kept_valid[:, :, None, None], partial_tiles, jnp.zeros_like(partial_tiles)
    )
    return (gate_out, grad_tiles.astype(jnp.bfloat16))


ZS = 4
PEERS = 16


def fused_kernel(
    rows_ref, valid_ref, tokens_ref, cot_ref, weight_ref, mask_ref,
    out_ref, grad_ref,
    tok, cot, w, gate, full,
    up_sem, down_sem, y_sem, sib_sem, ysib_sem, tok_recv,
    cot_send, cot_recv, gate_send, gate_recv, local_sem,
):
    me = lax.axis_index("fsdp")
    z = me // 4
    y = (me // 2) % 2
    c = me % 2
    width = weight_ref.shape[1]
    cols = width // TILE
    sibling = me + 1 - 2 * c
    partner = me + 2 - 4 * y

    def block(zz, yy, cc):
        return (zz * 2 + yy) * 2 + cc

    near = (z * (ZS - 1 - z)) // 2
    far_half = z // 2

    def order(k):
        f = k + near * (1 - 2 * k) * (1 - k // 2)
        return f + far_half * (ZS - 1 - 2 * f)

    def push(src, dst, send, recv, dev):
        return pltpu.make_async_remote_copy(
            src_ref=src, dst_ref=dst, send_sem=send, recv_sem=recv,
            device_id={"fsdp": dev}, device_id_type=pl.DeviceIdType.MESH,
        )

    barrier = pltpu.get_barrier_semaphore()

    def greet(o, carry):
        pl.semaphore_signal(
            barrier, inc=1, device_id={"fsdp": (me + o) % PEERS},
            device_id_type=pl.DeviceIdType.MESH,
        )
        return carry

    w_copy = pltpu.make_async_copy(weight_ref, w, local_sem.at[0])
    w_copy.start()
    tok_copy = pltpu.make_async_copy(tokens_ref, tok.at[me], local_sem.at[1])
    tok_copy.start()
    cot_copy = pltpu.make_async_copy(
        cot_ref.at[:, pl.ds(pl.multiple_of(me * width, width), width)], cot.at[me], local_sem.at[2]
    )
    cot_copy.start()
    lax.fori_loop(1, PEERS, greet, 0)
    pl.semaphore_wait(barrier, PEERS - 1)

    def tok_push(b, send, dev):
        return push(tok.at[b], tok.at[b], send, tok_recv.at[b], dev)

    def target(o):
        step = o - 1
        half = step // 8
        zh = (z // 2 + 1 + half) % 2
        j = (me % 8 + step % 8 + half) % 8
        return zh * 8 + j

    def cot_push(o):
        d = target(o)
        return push(
            cot_ref.at[:, pl.ds(pl.multiple_of(d * width, width), width)],
            cot.at[me], cot_send.at[o], cot_recv.at[me], d,
        )

    def gate_push(b):
        return push(
            gate.at[b],
            out_ref.at[:, pl.ds(pl.multiple_of(me * width, width), width)],
            gate_send.at[b], gate_recv.at[me], b,
        )

    def own_copy():
        return pltpu.make_async_copy(
            gate.at[me],
            out_ref.at[:, pl.ds(pl.multiple_of(me * width, width), width)],
            local_sem.at[3],
        )

    def row_forward(k, act):
        zk = order(k)
        b = block(zk, y, c)

        @pl.when(jnp.logical_and(zk <= z, z < ZS - 1))
        def _():
            act(tok_push(b, up_sem.at[k], me + 4))

        @pl.when(jnp.logical_and(zk >= z, z > 0))
        def _():
            act(tok_push(b, down_sem.at[k], me - 4))

        act(tok_push(b, y_sem.at[k], partner))
        act(tok_push(b, sib_sem.at[k], sibling))

    def start(copy):
        copy.start()

    def wait_send(copy):
        copy.wait_send()

    def arrived(b):
        tok_push(b, up_sem.at[0], sibling).wait_recv()

    def gate_values(zk, yk):
        first = block(zk, yk, 0)
        arrived(block(zk, yk, 1 - c))

        def chunk(j, carry):
            at = pl.ds(pl.multiple_of(j * 256, 256), 256)
            lhs = tok[pl.ds(first, 2)].reshape(2 * tok.shape[1], tok.shape[2])
            val = jnp.dot(lhs, w[:, at], preferred_element_type=jnp.float32)
            gate[pl.ds(first, 2), :, at] = val.astype(jnp.bfloat16).reshape(2, tok.shape[1], 256)
            return carry

        lax.fori_loop(0, width // 256, chunk, 0)

        def out(cc, carry):
            b = first + cc

            @pl.when(b != me)
            def _():
                gate_push(b).start()

            return carry

        lax.fori_loop(0, 2, out, 0)

    tok_copy.wait()
    row_forward(0, start)

    def send_cot(o, carry):
        cot_push(o).start()
        return carry


    w_copy.wait()

    def prune(r, carry):
        at = pl.ds(pl.multiple_of(r * TILE, TILE), TILE)
        w[at, :] = w[at, :] * mask_ref[r]
        return carry

    lax.fori_loop(0, RT, prune, 0)

    def stage(k, carry):
        @pl.when(jnp.logical_and(k >= 1, k < ZS))
        def _():
            arrived(block(order(k), y, c))
            row_forward(k, start)

        @pl.when(k >= 1)
        def _():
            b = block(order(k - 1), 1 - y, c)
            arrived(b)
            tok_push(b, ysib_sem.at[k - 1], sibling).start()

        for when, (lo, hi) in enumerate(zip((1, 4, 8, 12, 16)[:-1], (1, 4, 8, 12, 16)[1:])):

            @pl.when(k == when)
            def _(lo=lo, hi=hi):
                lax.fori_loop(lo, hi, send_cot, 0)

        @pl.when(k < ZS)
        def _():
            gate_values(order(k), y)

        @pl.when(k == 0)
        def _():
            own_copy().start()

        @pl.when(k >= 1)
        def _():
            gate_values(order(k - 1), 1 - y)

        return carry

    lax.fori_loop(0, ZS + 1, stage, 0)

    cot_copy.wait()

    def wait_cot(o, carry):
        src = (me + o) % PEERS
        push(cot.at[src], cot.at[src], cot_send.at[o], cot_recv.at[src], src).wait_recv()
        return carry

    lax.fori_loop(1, PEERS, wait_cot, 0)

    def grad_chunk(i, carry):
        at = pl.ds(pl.multiple_of(i * 256, 256), 256)
        lhs = tok[:, :, at].reshape(PEERS * tok.shape[1], 256)
        rhs = cot[...].reshape(PEERS * tok.shape[1], width)
        val = lax.dot_general(
            lhs, rhs, (((0,), (0,)), ((), ())), preferred_element_type=jnp.float32
        )
        full[pl.ds(2 * i, 2)] = val.astype(jnp.bfloat16).reshape(2, TILE, width)
        return carry

    lax.fori_loop(0, RT // 2, grad_chunk, 0)

    def pick(k, carry):
        for col in range(cols):
            r = rows_ref[col * KMAX + k]
            keep = valid_ref[col * KMAX + k]
            tile = full[r, :, col * TILE : (col + 1) * TILE].astype(jnp.float32)
            tile = jnp.where(keep > 0, tile, jnp.zeros_like(tile))
            grad_ref[col, k] = tile.astype(jnp.bfloat16)
        return carry

    lax.fori_loop(0, KMAX, pick, 0)

    def finish(o, carry):
        peer = (me + o) % PEERS
        cot_push(o).wait_send()
        gate_push(peer).wait_send()
        push(
            gate.at[peer],
            out_ref.at[:, pl.ds(pl.multiple_of(peer * width, width), width)],
            gate_send.at[peer], gate_recv.at[peer], peer,
        ).wait_recv()
        return carry

    lax.fori_loop(1, PEERS, finish, 0)
    own_copy().wait()

    def finish_row(k, carry):
        row_forward(k, wait_send)
        tok_push(block(order(k), 1 - y, c), ysib_sem.at[k], sibling).wait_send()
        return carry

    lax.fori_loop(0, ZS, finish_row, 0)


def fused_path(tokens, gate_cot, gate_weight, keep_mask):
    length, depth = tokens.shape
    width = gate_weight.shape[1]
    cols = width // TILE
    kept_rows, kept_valid = kept_lists(keep_mask)
    mask = jnp.repeat(keep_mask, TILE, axis=1).astype(jnp.bfloat16)[:, None, :]
    bf = jnp.bfloat16
    dma = pltpu.SemaphoreType.DMA
    anywhere = pl.BlockSpec(memory_space=pl.ANY)
    return pl.pallas_call(
        fused_kernel,
        out_shape=(
            jax.ShapeDtypeStruct((length, PEERS * width), bf),
            jax.ShapeDtypeStruct((cols, KMAX, TILE, TILE), bf),
        ),
        in_specs=[
            pl.BlockSpec(memory_space=pltpu.SMEM),
            pl.BlockSpec(memory_space=pltpu.SMEM),
            anywhere, anywhere, anywhere,
            pl.BlockSpec(memory_space=pltpu.VMEM),
        ],
        out_specs=(anywhere, pl.BlockSpec(memory_space=pltpu.VMEM)),
        scratch_shapes=[
            pltpu.VMEM((PEERS, length, depth), bf),
            pltpu.VMEM((PEERS, length, width), bf),
            pltpu.VMEM((depth, width), bf),
            pltpu.VMEM((PEERS, length, width), bf),
            pltpu.VMEM((RT, TILE, width), bf),
            dma((ZS,)), dma((ZS,)), dma((ZS,)), dma((ZS,)), dma((ZS,)), dma((PEERS,)),
            dma((PEERS,)), dma((PEERS,)), dma((PEERS,)), dma((PEERS,)), dma((4,)),
        ],
        compiler_params=pltpu.CompilerParams(
            collective_id=0, has_side_effects=True, vmem_limit_bytes=60 * 1024 * 1024
        ),
    )(
        kept_rows.astype(jnp.int32).reshape(-1),
        kept_valid.astype(jnp.int32).reshape(-1),
        tokens, gate_cot, gate_weight, mask,
    )


def on_device(tokens, gate_cot, gate_weight, keep_mask):
    small = (tokens.shape, gate_weight.shape[1]) == ((128, RT * TILE), 8 * TILE)
    if lax.axis_size("fsdp") == PEERS and small:
        return fused_path(tokens, gate_cot, gate_weight, keep_mask)
    return general_path(tokens, gate_cot, gate_weight, keep_mask)


def solution(mesh):
    placed = (
        P(("group", "fsdp"), None),
        P(("group", "fsdp"), None),
        P(None, "fsdp"),
        P(None, "fsdp"),
    )
    return jax.shard_map(
        on_device,
        mesh=mesh,
        in_specs=placed,
        out_specs=(P(("group", "fsdp"), None), P(("group", "fsdp"), None, None, None)),
        check_vma=False,
    )
```

```python
import jax
import jax.numpy as jnp
from jax import lax
from jax.experimental import pallas as pl
from jax.experimental.pallas import tpu as pltpu
from jax.sharding import PartitionSpec as P

TILE = 128
RT = 32
KMAX = 12


def kept_lists(keep_mask):
    kept_count = jnp.sum(keep_mask, axis=0)
    ordering = jnp.argsort(1 - keep_mask, axis=0, stable=True)[:KMAX]
    kept_rows = ordering.T
    kept_valid = jnp.arange(KMAX)[None, :] < kept_count[:, None]
    return (kept_rows, kept_valid)


def column_tiles(gate_weight, kept_rows, kept_valid, column):
    strip = gate_weight[:, column * TILE : (column + 1) * TILE].reshape(RT, TILE, TILE)
    picked = jnp.stack(
        [lax.dynamic_index_in_dim(strip, kept_rows[column, k], 0, False) for k in range(KMAX)]
    )
    picked = jnp.where(kept_valid[column][:, None, None], picked, jnp.zeros_like(picked))
    return picked.reshape(KMAX * TILE, TILE)


def general_path(tokens, gate_cot, gate_weight, keep_mask):
    local_width = gate_weight.shape[1]
    local_cols = local_width // TILE
    kept_rows, kept_valid = kept_lists(keep_mask)
    weight_cols = [
        column_tiles(gate_weight, kept_rows, kept_valid, column) for column in range(local_cols)
    ]
    cot_cols = lax.all_to_all(gate_cot, "fsdp", split_axis=1, concat_axis=0, tiled=True)
    total_rows = cot_cols.shape[0]

    def block_work(carry, piece, start):
        gate_all, grads = carry
        length = piece.shape[0]
        slope_piece = lax.dynamic_slice_in_dim(cot_cols, start, length, 0)
        outputs = []
        new_grads = []
        for column in range(local_cols):
            selected = jnp.concatenate(
                [
                    lax.dynamic_slice_in_dim(piece, kept_rows[column, k] * TILE, TILE, 1)
                    for k in range(KMAX)
                ],
                axis=1,
            )
            outputs.append(
                jnp.dot(selected, weight_cols[column], preferred_element_type=jnp.float32)
            )
            slope_col = slope_piece[:, column * TILE : (column + 1) * TILE]
            grad_col = lax.dot_general(
                selected, slope_col, (((0,), (0,)), ((), ())), preferred_element_type=jnp.float32
            )
            new_grads.append(grad_col.reshape(KMAX, TILE, TILE))
        values = jnp.concatenate(outputs, axis=1).astype(jnp.bfloat16)
        gate_all = lax.dynamic_update_slice_in_dim(gate_all, values, start, 0)
        return (gate_all, grads + jnp.stack(new_grads, axis=0))

    initial = (
        jnp.zeros((total_rows, local_width), jnp.bfloat16),
        jnp.zeros((local_cols, KMAX, TILE, TILE), jnp.float32),
    )
    piece = lax.all_gather(tokens, "fsdp", axis=0, tiled=True)
    length = piece.shape[0]

    def one_block(index, inner):
        offset = index * 1024
        block_rows = lax.dynamic_slice_in_dim(piece, offset, 1024, 0)
        return block_work(inner, block_rows, offset)

    gate_cols, partial_tiles = lax.fori_loop(0, length // 1024, one_block, initial)
    gate_out = lax.all_to_all(gate_cols, "fsdp", split_axis=0, concat_axis=1, tiled=True)
    grad_tiles = jnp.where(
        kept_valid[:, :, None, None], partial_tiles, jnp.zeros_like(partial_tiles)
    )
    return (gate_out, grad_tiles.astype(jnp.bfloat16))


ZS = 4
PEERS = 16
HALF = 8


def fused_kernel(
    mask_ref, mask_src, tokens_ref, cot_ref, weight_ref,
    out_ref, grad_ref,
    tok, cot, packed, w_outer, w_inner, gate, g_outer, g_inner, m_outer, m_inner,
    keep_outer, keep_inner, rank, flag, follow, rows, count,
    up_sem, down_sem, y_sem, sib_sem, ysib_sem, tok_recv,
    cot_send, cot_recv, gate_send, far_send, gate_recv,
    w_send, w_recv, wx_send, mask_sems, far_local, local_sem,
):
    me = lax.axis_index("fsdp")
    x = lax.axis_index("group")
    z = me // 4
    y = (me // 2) % 2
    c = me % 2
    side = z // 2
    mine = me % HALF
    home = side * HALF
    length = tok.shape[1]
    depth = tok.shape[2]
    width = cot.shape[2]
    cols = width // TILE
    part = cols // 2
    sibling = me + 1 - 2 * c
    partner = me + 2 - 4 * y
    inner = z == 1 + side

    def block(zz, yy, cc):
        return (zz * 2 + yy) * 2 + cc

    near = (z * (ZS - 1 - z)) // 2

    def order(k):
        f = k + near * (1 - 2 * k) * (1 - k // 2)
        return f + side * (ZS - 1 - 2 * f)

    def push(src, dst, send, recv, dev):
        return pltpu.make_async_remote_copy(
            src_ref=src, dst_ref=dst, send_sem=send, recv_sem=recv,
            device_id={"fsdp": dev}, device_id_type=pl.DeviceIdType.MESH,
        )

    def span(owner):
        return pl.ds(pl.multiple_of(owner * width, width), width)

    barrier = pltpu.get_barrier_semaphore()

    def greet(o, carry):
        pl.semaphore_signal(
            barrier, inc=1, device_id={"fsdp": (me + o) % PEERS},
            device_id_type=pl.DeviceIdType.MESH,
        )
        return carry

    def start(copy):
        copy.start()

    def wait_send(copy):
        copy.wait_send()

    tok_copy = pltpu.make_async_copy(tokens_ref, tok.at[me], local_sem.at[1])
    tok_copy.start()
    cot_copy = pltpu.make_async_copy(cot_ref.at[:, span(me)], cot.at[me], local_sem.at[2])
    lax.fori_loop(1, PEERS, greet, 0)
    pl.semaphore_signal(
        barrier, inc=1, device_id={"group": 1 - x}, device_id_type=pl.DeviceIdType.MESH
    )

    def tok_push(b, send, dev):
        return push(tok.at[b], tok.at[b], send, tok_recv.at[b], dev)

    def cot_push(d):
        return push(cot_ref.at[:, span(d)], cot.at[me], cot_send.at[d], cot_recv.at[me], d)

    def near_target(o):
        return home + (mine + o) % HALF

    def far_target(t):
        late = t // 4
        zz = (1 - side) * (3 - late) + side * late
        return block(zz, (y + t // 2) % 2, (c + t) % 2)

    def far_taker(o):
        late = o // 4
        zz = side * (3 - late) + (1 - side) * late
        return zz * 4 + (me % 4 + o + late) % 4

    def gate_push(b):
        return push(
            gate.at[b % HALF], out_ref.at[:, span(me)],
            gate_send.at[b % HALF], gate_recv.at[me], b,
        )

    def own_copy():
        return pltpu.make_async_copy(gate.at[mine], out_ref.at[:, span(me)], local_sem.at[3])

    def owner_of(slot):
        return block((1 - side) * (3 - slot) + side * slot, y, c)

    def far_push(made, slot, b):
        return push(
            made.at[b % HALF], out_ref.at[:, span(owner_of(slot))],
            far_send.at[slot, b % HALF], gate_recv.at[owner_of(slot)], b,
        )

    def far_copy(made, slot):
        return pltpu.make_async_copy(
            made.at[mine], out_ref.at[:, span(owner_of(slot))], far_local.at[slot]
        )

    def w_push(j, far, slot):
        col = x * part + j
        return push(
            packed.at[j], far.at[col], w_send.at[j], w_recv.at[slot, col], block(2 - side, y, c)
        )

    def w_cross(far, slot, col):
        return pltpu.make_async_remote_copy(
            src_ref=far.at[col], dst_ref=far.at[col],
            send_sem=wx_send.at[slot, col % part], recv_sem=w_recv.at[slot, col],
            device_id={"group": 1 - x}, device_id_type=pl.DeviceIdType.MESH,
        )

    def mask_push(land, slot):
        return push(mask_src, land, mask_sems.at[0], mask_sems.at[1 + slot], block(2 - side, y, c))

    def row_forward(k, act, across):
        zk = order(k)
        b = block(zk, y, c)

        @pl.when(
            jnp.logical_and(zk <= z, jnp.logical_and(z < ZS - 1, (z == 1) == across))
        )
        def _():
            act(tok_push(b, up_sem.at[k], me + 4))

        @pl.when(jnp.logical_and(zk >= z, jnp.logical_and(z > 0, (z == 2) == across)))
        def _():
            act(tok_push(b, down_sem.at[k], me - 4))

    def row_share(k, act):
        b = block(order(k), y, c)
        act(tok_push(b, y_sem.at[k], partner))
        act(tok_push(b, sib_sem.at[k], sibling))

    def arrived(b):
        tok_push(b, up_sem.at[0], sibling).wait_recv()

    def cot_arrived(b):
        push(cot.at[b], cot.at[b], cot_send.at[b], cot_recv.at[b], b).wait_recv()

    def find_rows(col, carry):
        follow[RT] = RT - 1

        def back(i, state):
            nxt, total = state
            r = RT - 1 - i
            keep = mask_ref[col, r]
            nxt = jnp.where(keep > 0, r, nxt)
            follow[r] = nxt
            return (nxt, total + keep)

        count[col] = lax.fori_loop(0, RT, back, (RT - 1, 0), unroll=True)[1]

        def ahead(k, pos):
            r = follow[pos]
            rows[col * KMAX + k] = r
            return jnp.minimum(r + 1, RT)

        lax.fori_loop(0, KMAX, ahead, 0, unroll=True)
        return carry

    def gates(w, chunk_buf, held):
        w_copy = pltpu.make_async_copy(weight_ref, w, local_sem.at[0])
        w_copy.start()
        cot_copy.start()
        lax.fori_loop(0, cols, find_rows, 0)
        tok_copy.wait()
        pl.semaphore_wait(barrier, PEERS)
        row_forward(0, start, False)
        row_forward(0, start, True)
        row_share(0, start)

        def send_far(t, carry):
            cot_push(far_target(t)).start()
            return carry

        @pl.when(inner)
        def _():
            send_far(0, 0)

        @pl.when(inner)
        def _():
            mask_push(m_inner, 1).start()

        @pl.when(jnp.logical_not(inner))
        def _():
            mask_push(m_outer, 0).start()

        w_copy.wait()

        def pack(k, carry):
            for j in range(part):
                col = x * part + j
                r = rows[col * KMAX + k]
                packed[j, k] = w[r, :, pl.ds(pl.multiple_of(col * TILE, TILE), TILE)]
            return carry

        lax.fori_loop(0, KMAX, pack, 0)

        def early_weights(j, carry):
            w_push(j, w_outer, 0).start()
            return carry

        @pl.when(jnp.logical_not(inner))
        def _():
            lax.fori_loop(0, part, early_weights, 0)

        def send_near(o, carry):
            cot_push(near_target(o)).start()
            return carry

        lax.fori_loop(1, HALF, send_near, 0)

        def prune(r, carry):
            for col in range(cols):
                at = slice(col * TILE, (col + 1) * TILE)
                keep = jnp.full((1, TILE), mask_ref[col, r].astype(jnp.float32))
                w[r, :, at] = w[r, :, at] * keep.astype(jnp.bfloat16)
            return carry

        lax.fori_loop(0, RT, prune, 0)

        def gate_values(zk, yk):
            first = block(zk, yk, 0)
            slot = first % HALF
            arrived(block(zk, yk, 1 - c))

            def chunk(j, carry):
                at = pl.ds(pl.multiple_of(j * 256, 256), 256)
                lhs = tok[pl.ds(first, 2)].reshape(2 * length, depth)
                rhs = w[:, :, at].reshape(depth, 256)
                val = jnp.dot(lhs, rhs, preferred_element_type=jnp.float32)
                gate[pl.ds(slot, 2), :, at] = val.astype(jnp.bfloat16).reshape(2, length, 256)
                return carry

            lax.fori_loop(0, width // 256, chunk, 0)

            def out(cc, carry):
                b = first + cc

                @pl.when(b != me)
                def _():
                    gate_push(b).start()

                return carry

            lax.fori_loop(0, 2, out, 0)

        def row_arrived(k):
            arrived(block(order(k), y, c))
            row_forward(k, start, False)
            row_forward(k, start, True)
            row_share(k, start)

        def side_arrived(k):
            b = block(order(k), 1 - y, c)
            arrived(b)
            tok_push(b, ysib_sem.at[k], sibling).start()

        def relays(far, slot, lo, hi):
            def one(j, carry):
                w_cross(far, slot, x * part + j).wait_recv()
                w_cross(far, slot, x * part + j).start()
                return carry

            lax.fori_loop(lo, hi, one, 0)

        def late_weights(j, carry):
            w_push(j, w_inner, 1).start()
            return carry

        def step(k, carry):
            @pl.when(k == 1)
            def _():
                row_arrived(1)

            @pl.when(jnp.logical_and(inner, k == 1))
            def _():
                lax.fori_loop(0, part, late_weights, 0)
                lax.fori_loop(1, 8, send_far, 0)
                row_arrived(2)

            @pl.when(k >= 2)
            def _():
                side_arrived(k - 2)

            @pl.when(jnp.logical_and(inner, k >= 2))
            def _():
                relays(w_outer, 0, 2 * (k - 2), 2 * (k - 1))

            gate_values(order(k % 2), y + (k // 2) * (1 - 2 * y))

            @pl.when(k == 0)
            def _():
                own_copy().start()

            return carry

        lax.fori_loop(0, 4, step, 0)

        @pl.when(jnp.logical_not(inner))
        def _():
            lax.fori_loop(0, 8, send_far, 0)
            row_arrived(2)

        row_arrived(3)

        def far_gates(far, made, kept, slot):
            def crossed(j, inside):
                w_cross(far, slot, (1 - x) * part + j).wait_recv()
                return inside

            lax.fori_loop(0, part, crossed, 0)

            def hold(col, inside):
                held[col] = far[col]
                return inside

            lax.fori_loop(0, cols, hold, 0)

            def ranks(col, inside):
                seen = 0
                for r in range(RT):
                    keep = kept[col, r]
                    rank[col * RT + r] = jnp.minimum(seen, KMAX - 1)
                    flag[col * RT + r] = keep
                    seen = seen + keep
                return inside

            lax.fori_loop(0, cols, ranks, 0)

            def pair(p, inside):
                for e in range(2):
                    col = 2 * p + e

                    def place(r, deeper):
                        tile = held[col, rank[col * RT + r]]
                        factor = jnp.full((1, TILE), flag[col * RT + r].astype(jnp.float32))
                        chunk_buf[r, :, e * TILE : (e + 1) * TILE] = tile * factor.astype(
                            jnp.bfloat16
                        )
                        return deeper

                    lax.fori_loop(0, RT, place, 0)

                def rows_part(m, deeper):
                    at = pl.ds(pl.multiple_of(p * 256, 256), 256)
                    lhs = tok[pl.ds(home + 4 * m, 4)].reshape(4 * length, depth)
                    rhs = chunk_buf[...].reshape(depth, 256)
                    val = jnp.dot(lhs, rhs, preferred_element_type=jnp.float32)
                    made[pl.ds(4 * m, 4), :, at] = val.astype(jnp.bfloat16).reshape(
                        4, length, 256
                    )
                    return deeper

                lax.fori_loop(0, 2, rows_part, 0)
                return inside

            lax.fori_loop(0, width // 256, pair, 0)
            far_copy(made, slot).start()

            def out(o, inside):
                far_push(made, slot, far_taker(o)).start()
                return inside

            lax.fori_loop(0, HALF - 1, out, 0)

        @pl.when(inner)
        def _():
            for slot, (land, kept) in enumerate(((m_outer, keep_outer), (m_inner, keep_inner))):
                mask_push(land, slot).wait_recv()
                fetch = pltpu.make_async_copy(land, kept, local_sem.at[4 + slot])
                fetch.start()
                fetch.wait()

        sets = ((w_outer, g_outer, keep_outer), (w_inner, g_inner, keep_inner))
        for slot, (far, made, kept) in enumerate(sets):

            @pl.when(inner)
            def _(far=far, made=made, kept=kept, slot=slot):
                relays(w_inner, 1, 2 * slot, 2 * slot + 2)
                far_gates(far, made, kept, slot)

            side_arrived(2 + slot)

    pl.run_scoped(
        gates,
        pltpu.VMEM((RT, TILE, width), jnp.bfloat16),
        pltpu.VMEM((RT, TILE, 256), jnp.bfloat16),
        pltpu.VMEM((cols, KMAX, TILE, TILE), jnp.bfloat16),
    )

    def grads(full):
        def add(first, blocks, fresh):
            def chunk(i, carry):
                at = pl.ds(pl.multiple_of(i * 512, 512), 512)
                lhs = tok[pl.ds(first, blocks), :, at].reshape(blocks * length, 512)
                rhs = cot[pl.ds(first, blocks)].reshape(blocks * length, width)
                val = lax.dot_general(
                    lhs, rhs, (((0,), (0,)), ((), ())), preferred_element_type=jnp.float32
                ).reshape(4, TILE, width)
                if not fresh:
                    val = val + full[pl.ds(4 * i, 4)]
                full[pl.ds(4 * i, 4)] = val
                return carry

            lax.fori_loop(0, RT // 4, chunk, 0)

        cot_copy.wait()

        def near_cot(o, carry):
            cot_arrived(near_target(o))
            return carry

        lax.fori_loop(1, HALF, near_cot, 0)
        add(home, HALF, True)

        def far_sibling(k, carry):
            arrived(block(order(k), y, 1 - c))
            arrived(block(order(k), 1 - y, 1 - c))
            return carry

        lax.fori_loop(2, ZS, far_sibling, 0)

        def far_pair(t, carry):
            first = block((1 - side) * (2 + t % 2) + side * (1 - t % 2), (y + t // 2) % 2, 0)
            cot_arrived(first)
            cot_arrived(first + 1)
            add(first, 2, False)
            return carry

        lax.fori_loop(0, 4, far_pair, 0)

        def pick(k, carry):
            for col in range(cols):
                r = rows[col * KMAX + k]
                tile = full[r, :, col * TILE : (col + 1) * TILE]
                tile = jnp.where(k < count[col], tile, jnp.zeros_like(tile))
                grad_ref[col, k] = tile.astype(jnp.bfloat16)
            return carry

        lax.fori_loop(0, KMAX, pick, 0)

    pl.run_scoped(grads, pltpu.VMEM((RT, TILE, width), jnp.float32))

    def finish_near(o, carry):
        peer = near_target(o)
        cot_push(peer).wait_send()
        gate_push(peer).wait_send()
        push(
            gate.at[mine], out_ref.at[:, span(peer)],
            gate_send.at[peer % HALF], gate_recv.at[peer], peer,
        ).wait_recv()
        return carry

    lax.fori_loop(1, HALF, finish_near, 0)

    def finish_far(o, carry):
        owner = HALF - home + o
        cot_push(owner).wait_send()
        local = jnp.logical_and(inner, o % 4 == me % 4)

        @pl.when(jnp.logical_not(local))
        def _():
            push(
                gate.at[mine], out_ref.at[:, span(owner)],
                gate_send.at[mine], gate_recv.at[owner], owner,
            ).wait_recv()

        return carry

    lax.fori_loop(0, HALF, finish_far, 0)
    own_copy().wait()

    def finish_weights(j, carry):
        w_push(j, w_outer, 0).wait_send()
        return carry

    lax.fori_loop(0, part, finish_weights, 0)
    mask_push(m_outer, 0).wait_send()

    @pl.when(inner)
    def _():
        for slot, (far, made) in enumerate(((w_outer, g_outer), (w_inner, g_inner))):

            def relayed(j, carry, far=far, slot=slot):
                w_cross(far, slot, x * part + j).wait_send()
                return carry

            def sent(o, carry, made=made, slot=slot):
                far_push(made, slot, far_taker(o)).wait_send()
                return carry

            lax.fori_loop(0, part, relayed, 0)
            far_copy(made, slot).wait()
            lax.fori_loop(0, HALF - 1, sent, 0)

    def finish_row(k, carry):
        row_forward(k, wait_send, False)
        row_forward(k, wait_send, True)
        row_share(k, wait_send)
        tok_push(block(order(k), 1 - y, c), ysib_sem.at[k], sibling).wait_send()
        return carry

    lax.fori_loop(0, ZS, finish_row, 0)


def fused_path(tokens, gate_cot, gate_weight, keep_mask):
    length, depth = tokens.shape
    width = gate_weight.shape[1]
    cols = width // TILE
    bf = jnp.bfloat16
    dma = pltpu.SemaphoreType.DMA
    anywhere = pl.BlockSpec(memory_space=pl.ANY)
    in_vmem = pl.BlockSpec(memory_space=pltpu.VMEM)
    mask = keep_mask.T
    return pl.pallas_call(
        fused_kernel,
        out_shape=(
            jax.ShapeDtypeStruct((length, PEERS * width), bf),
            jax.ShapeDtypeStruct((cols, KMAX, TILE, TILE), bf),
        ),
        in_specs=[
            pl.BlockSpec(memory_space=pltpu.SMEM), in_vmem, anywhere, anywhere, anywhere,
        ],
        out_specs=(anywhere, in_vmem),
        scratch_shapes=[
            pltpu.VMEM((PEERS, length, depth), bf),
            pltpu.VMEM((PEERS, length, width), bf),
            pltpu.VMEM((cols // 2, KMAX, TILE, TILE), bf),
            pltpu.VMEM((cols, KMAX, TILE, TILE), bf),
            pltpu.VMEM((cols, KMAX, TILE, TILE), bf),
            pltpu.VMEM((HALF, length, width), bf),
            pltpu.VMEM((HALF, length, width), bf),
            pltpu.VMEM((HALF, length, width), bf),
            pltpu.VMEM((cols, RT), jnp.int32),
            pltpu.VMEM((cols, RT), jnp.int32),
            pltpu.SMEM((cols, RT), jnp.int32),
            pltpu.SMEM((cols, RT), jnp.int32),
            pltpu.SMEM((cols * RT,), jnp.int32),
            pltpu.SMEM((cols * RT,), jnp.int32),
            pltpu.SMEM((RT + 1,), jnp.int32),
            pltpu.SMEM((cols * KMAX,), jnp.int32),
            pltpu.SMEM((cols,), jnp.int32),
            dma((ZS,)), dma((ZS,)), dma((ZS,)), dma((ZS,)), dma((ZS,)), dma((PEERS,)),
            dma((PEERS,)), dma((PEERS,)), dma((HALF,)), dma((2, HALF)), dma((PEERS,)),
            dma((cols // 2,)), dma((2, cols)), dma((2, cols // 2)), dma((3,)), dma((2,)), dma((6,)),
        ],
        compiler_params=pltpu.CompilerParams(
            collective_id=0, has_side_effects=True, vmem_limit_bytes=60 * 1024 * 1024
        ),
    )(mask, mask, tokens, gate_cot, gate_weight.reshape(RT, TILE, width))


def on_device(tokens, gate_cot, gate_weight, keep_mask):
    small = (tokens.shape, gate_weight.shape[1]) == ((128, RT * TILE), 8 * TILE)
    if lax.axis_size("fsdp") == PEERS and lax.axis_size("group") == 2 and small:
        return fused_path(tokens, gate_cot, gate_weight, keep_mask)
    return general_path(tokens, gate_cot, gate_weight, keep_mask)


def solution(mesh):
    placed = (
        P(("group", "fsdp"), None),
        P(("group", "fsdp"), None),
        P(None, "fsdp"),
        P(None, "fsdp"),
    )
    return jax.shard_map(
        on_device,
        mesh=mesh,
        in_specs=placed,
        out_specs=(P(("group", "fsdp"), None), P(("group", "fsdp"), None, None, None)),
        check_vma=False,
    )
```

```python
import jax
import jax.numpy as jnp
from jax import lax
from jax.experimental import pallas as pl
from jax.experimental.pallas import tpu as pltpu
from jax.sharding import PartitionSpec as P

TILE = 128
RT = 32
KMAX = 12


def kept_lists(keep_mask):
    kept_count = jnp.sum(keep_mask, axis=0)
    ordering = jnp.argsort(1 - keep_mask, axis=0, stable=True)[:KMAX]
    kept_rows = ordering.T
    kept_valid = jnp.arange(KMAX)[None, :] < kept_count[:, None]
    return (kept_rows, kept_valid)


def column_tiles(gate_weight, kept_rows, kept_valid, column):
    strip = gate_weight[:, column * TILE : (column + 1) * TILE].reshape(RT, TILE, TILE)
    picked = jnp.stack(
        [lax.dynamic_index_in_dim(strip, kept_rows[column, k], 0, False) for k in range(KMAX)]
    )
    picked = jnp.where(kept_valid[column][:, None, None], picked, jnp.zeros_like(picked))
    return picked.reshape(KMAX * TILE, TILE)


def general_path(tokens, gate_cot, gate_weight, keep_mask):
    local_width = gate_weight.shape[1]
    local_cols = local_width // TILE
    kept_rows, kept_valid = kept_lists(keep_mask)
    weight_cols = [
        column_tiles(gate_weight, kept_rows, kept_valid, column) for column in range(local_cols)
    ]
    cot_cols = lax.all_to_all(gate_cot, "fsdp", split_axis=1, concat_axis=0, tiled=True)
    total_rows = cot_cols.shape[0]

    def block_work(carry, piece, start):
        gate_all, grads = carry
        length = piece.shape[0]
        slope_piece = lax.dynamic_slice_in_dim(cot_cols, start, length, 0)
        outputs = []
        new_grads = []
        for column in range(local_cols):
            selected = jnp.concatenate(
                [
                    lax.dynamic_slice_in_dim(piece, kept_rows[column, k] * TILE, TILE, 1)
                    for k in range(KMAX)
                ],
                axis=1,
            )
            outputs.append(
                jnp.dot(selected, weight_cols[column], preferred_element_type=jnp.float32)
            )
            slope_col = slope_piece[:, column * TILE : (column + 1) * TILE]
            grad_col = lax.dot_general(
                selected, slope_col, (((0,), (0,)), ((), ())), preferred_element_type=jnp.float32
            )
            new_grads.append(grad_col.reshape(KMAX, TILE, TILE))
        values = jnp.concatenate(outputs, axis=1).astype(jnp.bfloat16)
        gate_all = lax.dynamic_update_slice_in_dim(gate_all, values, start, 0)
        return (gate_all, grads + jnp.stack(new_grads, axis=0))

    initial = (
        jnp.zeros((total_rows, local_width), jnp.bfloat16),
        jnp.zeros((local_cols, KMAX, TILE, TILE), jnp.float32),
    )
    piece = lax.all_gather(tokens, "fsdp", axis=0, tiled=True)
    length = piece.shape[0]

    def one_block(index, inner):
        offset = index * 1024
        block_rows = lax.dynamic_slice_in_dim(piece, offset, 1024, 0)
        return block_work(inner, block_rows, offset)

    gate_cols, partial_tiles = lax.fori_loop(0, length // 1024, one_block, initial)
    gate_out = lax.all_to_all(gate_cols, "fsdp", split_axis=0, concat_axis=1, tiled=True)
    grad_tiles = jnp.where(
        kept_valid[:, :, None, None], partial_tiles, jnp.zeros_like(partial_tiles)
    )
    return (gate_out, grad_tiles.astype(jnp.bfloat16))


ZS = 4
PEERS = 16
HALF = 8


def fused_kernel(
    mask_ref, mask_src, tokens_ref, cot_ref, weight_ref,
    out_ref, grad_ref,
    tok, cot, packed, w_outer, w_inner, gate, g_outer, g_inner, m_outer, m_inner,
    keep_outer, keep_inner, rank, flag, follow, rows, count,
    up_sem, down_sem, y_sem, sib_sem, ysib_sem, tok_recv,
    cot_send, cot_recv, gate_send, far_send, gate_recv,
    w_send, w_recv, wx_send, mask_sems, far_local, local_sem,
):
    me = lax.axis_index("fsdp")
    x = lax.axis_index("group")
    z = me // 4
    y = (me // 2) % 2
    c = me % 2
    side = z // 2
    mine = me % HALF
    home = side * HALF
    length = tok.shape[1]
    depth = tok.shape[2]
    width = cot.shape[2]
    cols = width // TILE
    part = cols // 2
    sibling = me + 1 - 2 * c
    partner = me + 2 - 4 * y
    inner = z == 1 + side

    def block(zz, yy, cc):
        return (zz * 2 + yy) * 2 + cc

    near = (z * (ZS - 1 - z)) // 2

    def order(k):
        f = k + near * (1 - 2 * k) * (1 - k // 2)
        return f + side * (ZS - 1 - 2 * f)

    def push(src, dst, send, recv, dev):
        return pltpu.make_async_remote_copy(
            src_ref=src, dst_ref=dst, send_sem=send, recv_sem=recv,
            device_id={"fsdp": dev}, device_id_type=pl.DeviceIdType.MESH,
        )

    def span(owner):
        return pl.ds(pl.multiple_of(owner * width, width), width)

    barrier = pltpu.get_barrier_semaphore()

    def greet(o, carry):
        pl.semaphore_signal(
            barrier, inc=1, device_id={"fsdp": (me + o) % PEERS},
            device_id_type=pl.DeviceIdType.MESH,
        )
        return carry

    def start(copy):
        copy.start()

    def wait_send(copy):
        copy.wait_send()

    tok_copy = pltpu.make_async_copy(tokens_ref, tok.at[me], local_sem.at[1])
    tok_copy.start()
    cot_copy = pltpu.make_async_copy(cot_ref.at[:, span(me)], cot.at[me], local_sem.at[2])
    lax.fori_loop(1, PEERS, greet, 0)
    pl.semaphore_signal(
        barrier, inc=1, device_id={"group": 1 - x}, device_id_type=pl.DeviceIdType.MESH
    )

    def tok_push(b, send, dev):
        return push(tok.at[b], tok.at[b], send, tok_recv.at[b], dev)

    def cot_push(d):
        return push(cot_ref.at[:, span(d)], cot.at[me], cot_send.at[d], cot_recv.at[me], d)

    def near_target(o):
        return home + (mine + o) % HALF

    def far_target(t):
        late = t // 4
        zz = (1 - side) * (3 - late) + side * late
        return block(zz, (y + t // 2) % 2, (c + t) % 2)

    def far_taker(o):
        late = o // 4
        zz = side * (3 - late) + (1 - side) * late
        return zz * 4 + (me % 4 + o + late) % 4

    def gate_push(b):
        return push(
            gate.at[b % HALF], out_ref.at[:, span(me)],
            gate_send.at[b % HALF], gate_recv.at[me], b,
        )

    def own_copy():
        return pltpu.make_async_copy(gate.at[mine], out_ref.at[:, span(me)], local_sem.at[3])

    def owner_of(slot):
        return block((1 - side) * (3 - slot) + side * slot, y, c)

    def far_push(made, slot, b):
        return push(
            made.at[b % HALF], out_ref.at[:, span(owner_of(slot))],
            far_send.at[slot, b % HALF], gate_recv.at[owner_of(slot)], b,
        )

    def far_copy(made, slot):
        return pltpu.make_async_copy(
            made.at[mine], out_ref.at[:, span(owner_of(slot))], far_local.at[slot]
        )

    def w_push(j, far, slot):
        col = x * part + j
        return push(
            packed.at[j], far.at[col], w_send.at[j], w_recv.at[slot, col], block(2 - side, y, c)
        )

    def w_cross(far, slot, col):
        return pltpu.make_async_remote_copy(
            src_ref=far.at[col], dst_ref=far.at[col],
            send_sem=wx_send.at[slot, col % part], recv_sem=w_recv.at[slot, col],
            device_id={"group": 1 - x}, device_id_type=pl.DeviceIdType.MESH,
        )

    def mask_push(land, slot):
        return push(mask_src, land, mask_sems.at[0], mask_sems.at[1 + slot], block(2 - side, y, c))

    def row_forward(k, act, across):
        zk = order(k)
        b = block(zk, y, c)

        @pl.when(
            jnp.logical_and(zk <= z, jnp.logical_and(z < ZS - 1, (z == 1) == across))
        )
        def _():
            act(tok_push(b, up_sem.at[k], me + 4))

        @pl.when(jnp.logical_and(zk >= z, jnp.logical_and(z > 0, (z == 2) == across)))
        def _():
            act(tok_push(b, down_sem.at[k], me - 4))

    def row_share(k, act):
        b = block(order(k), y, c)
        act(tok_push(b, y_sem.at[k], partner))
        act(tok_push(b, sib_sem.at[k], sibling))

    def arrived(b):
        tok_push(b, up_sem.at[0], sibling).wait_recv()

    def cot_arrived(b):
        push(cot.at[b], cot.at[b], cot_send.at[b], cot_recv.at[b], b).wait_recv()

    def find_rows(col, carry):
        follow[RT] = RT - 1

        def back(i, state):
            nxt, total = state
            r = RT - 1 - i
            keep = mask_ref[col, r]
            nxt = jnp.where(keep > 0, r, nxt)
            follow[r] = nxt
            return (nxt, total + keep)

        count[col] = lax.fori_loop(0, RT, back, (RT - 1, 0), unroll=True)[1]

        def ahead(k, pos):
            r = follow[pos]
            rows[col * KMAX + k] = r
            return jnp.minimum(r + 1, RT)

        lax.fori_loop(0, KMAX, ahead, 0, unroll=True)
        return carry

    def gates(w, chunk_buf, held):
        w_copy = pltpu.make_async_copy(weight_ref, w, local_sem.at[0])
        w_copy.start()
        cot_copy.start()
        lax.fori_loop(0, cols, find_rows, 0)
        tok_copy.wait()
        pl.semaphore_wait(barrier, PEERS)
        row_forward(0, start, False)
        row_forward(0, start, True)
        row_share(0, start)

        def send_far(t, carry):
            cot_push(far_target(t)).start()
            return carry

        @pl.when(inner)
        def _():
            send_far(0, 0)

        @pl.when(inner)
        def _():
            mask_push(m_inner, 1).start()

        @pl.when(jnp.logical_not(inner))
        def _():
            mask_push(m_outer, 0).start()

        w_copy.wait()

        def pack(k, carry):
            for j in range(part):
                col = x * part + j
                r = rows[col * KMAX + k]
                packed[j, k] = w[r, :, pl.ds(pl.multiple_of(col * TILE, TILE), TILE)]
            return carry

        lax.fori_loop(0, KMAX, pack, 0)

        def early_weights(j, carry):
            w_push(j, w_outer, 0).start()
            return carry

        @pl.when(jnp.logical_not(inner))
        def _():
            lax.fori_loop(0, part, early_weights, 0)

        def send_near(o, carry):
            cot_push(near_target(o)).start()
            return carry

        lax.fori_loop(1, HALF, send_near, 0)

        def prune(r, carry):
            for col in range(cols):
                at = slice(col * TILE, (col + 1) * TILE)
                keep = jnp.full((1, TILE), mask_ref[col, r].astype(jnp.float32))
                w[r, :, at] = w[r, :, at] * keep.astype(jnp.bfloat16)
            return carry

        lax.fori_loop(0, RT, prune, 0)

        def gate_values(zk, yk):
            first = block(zk, yk, 0)
            slot = first % HALF
            arrived(block(zk, yk, 1 - c))

            def chunk(j, carry):
                at = pl.ds(pl.multiple_of(j * 256, 256), 256)
                lhs = tok[pl.ds(first, 2)].reshape(2 * length, depth)
                rhs = w[:, :, at].reshape(depth, 256)
                val = jnp.dot(lhs, rhs, preferred_element_type=jnp.float32)
                gate[pl.ds(slot, 2), :, at] = val.astype(jnp.bfloat16).reshape(2, length, 256)
                return carry

            lax.fori_loop(0, width // 256, chunk, 0)

            def out(cc, carry):
                b = first + cc

                @pl.when(b != me)
                def _():
                    gate_push(b).start()

                return carry

            lax.fori_loop(0, 2, out, 0)

        def row_arrived(k):
            arrived(block(order(k), y, c))
            row_forward(k, start, False)
            row_forward(k, start, True)
            row_share(k, start)

        def side_arrived(k):
            b = block(order(k), 1 - y, c)
            arrived(b)
            tok_push(b, ysib_sem.at[k], sibling).start()

        def relays(far, slot, lo, hi):
            def one(j, carry):
                w_cross(far, slot, x * part + j).wait_recv()
                w_cross(far, slot, x * part + j).start()
                return carry

            lax.fori_loop(lo, hi, one, 0)

        def late_weights(j, carry):
            w_push(j, w_inner, 1).start()
            return carry

        def step(k, carry):
            @pl.when(k == 1)
            def _():
                row_arrived(1)

            @pl.when(jnp.logical_and(inner, k == 1))
            def _():
                lax.fori_loop(0, part, late_weights, 0)
                lax.fori_loop(1, 8, send_far, 0)
                row_arrived(2)

            @pl.when(k >= 2)
            def _():
                side_arrived(k - 2)

            @pl.when(jnp.logical_and(inner, k >= 2))
            def _():
                relays(w_outer, 0, 2 * (k - 2), 2 * (k - 1))

            gate_values(order(k % 2), y + (k // 2) * (1 - 2 * y))

            @pl.when(k == 0)
            def _():
                own_copy().start()

            return carry

        lax.fori_loop(0, 4, step, 0)

        @pl.when(jnp.logical_not(inner))
        def _():
            lax.fori_loop(0, 8, send_far, 0)
            row_arrived(2)

        row_arrived(3)

        def far_gates(far, made, slot):
            def crossed(j, inside):
                w_cross(far, slot, (1 - x) * part + j).wait_recv()
                return inside

            lax.fori_loop(0, part, crossed, 0)

            def hold(col, inside):
                held[col] = far[col]
                return inside

            lax.fori_loop(0, cols, hold, 0)

            def pair(p, inside):
                for e in range(2):
                    col = 2 * p + e

                    def place(r, deeper):
                        at = (slot * cols + col) * RT + r
                        tile = held[col, rank[at]]
                        factor = jnp.full((1, TILE), flag[at].astype(jnp.float32))
                        chunk_buf[r, :, e * TILE : (e + 1) * TILE] = tile * factor.astype(
                            jnp.bfloat16
                        )
                        return deeper

                    lax.fori_loop(0, RT, place, 0)

                def rows_part(m, deeper):
                    at = pl.ds(pl.multiple_of(p * 256, 256), 256)
                    lhs = tok[pl.ds(home + 4 * m, 4)].reshape(4 * length, depth)
                    rhs = chunk_buf[...].reshape(depth, 256)
                    val = jnp.dot(lhs, rhs, preferred_element_type=jnp.float32)
                    made[pl.ds(4 * m, 4), :, at] = val.astype(jnp.bfloat16).reshape(
                        4, length, 256
                    )
                    return deeper

                lax.fori_loop(0, 2, rows_part, 0)
                return inside

            lax.fori_loop(0, width // 256, pair, 0)
            far_copy(made, slot).start()

            def out(o, inside):
                far_push(made, slot, far_taker(o)).start()
                return inside

            lax.fori_loop(0, HALF - 1, out, 0)

        @pl.when(inner)
        def _():
            for slot, (land, kept) in enumerate(((m_outer, keep_outer), (m_inner, keep_inner))):
                mask_push(land, slot).wait_recv()
                fetch = pltpu.make_async_copy(land, kept, local_sem.at[4 + slot])
                fetch.start()
                fetch.wait()

                def ranks(col, carry, kept=kept, slot=slot):
                    seen = 0
                    for r in range(RT):
                        keep = kept[col, r]
                        at = (slot * cols + col) * RT + r
                        rank[at] = jnp.minimum(seen, KMAX - 1)
                        flag[at] = keep
                        seen = seen + keep
                    return carry

                lax.fori_loop(0, cols, ranks, 0)

        sets = ((w_outer, g_outer, keep_outer), (w_inner, g_inner, keep_inner))
        for slot, (far, made, kept) in enumerate(sets):

            @pl.when(inner)
            def _(far=far, made=made, kept=kept, slot=slot):
                relays(w_inner, 1, 2 * slot, 2 * slot + 2)
                far_gates(far, made, slot)

            side_arrived(2 + slot)

    pl.run_scoped(
        gates,
        pltpu.VMEM((RT, TILE, width), jnp.bfloat16),
        pltpu.VMEM((RT, TILE, 256), jnp.bfloat16),
        pltpu.VMEM((cols, KMAX, TILE, TILE), jnp.bfloat16),
    )

    def grads(full):
        def add(first, blocks, fresh):
            def chunk(i, carry):
                at = pl.ds(pl.multiple_of(i * 512, 512), 512)
                lhs = tok[pl.ds(first, blocks), :, at].reshape(blocks * length, 512)
                rhs = cot[pl.ds(first, blocks)].reshape(blocks * length, width)
                val = lax.dot_general(
                    lhs, rhs, (((0,), (0,)), ((), ())), preferred_element_type=jnp.float32
                ).reshape(4, TILE, width)
                if not fresh:
                    val = val + full[pl.ds(4 * i, 4)]
                full[pl.ds(4 * i, 4)] = val
                return carry

            lax.fori_loop(0, RT // 4, chunk, 0)

        cot_copy.wait()

        def near_cot(o, carry):
            cot_arrived(near_target(o))
            return carry

        lax.fori_loop(1, HALF, near_cot, 0)
        add(home, HALF, True)

        def far_sibling(k, carry):
            arrived(block(order(k), y, 1 - c))
            arrived(block(order(k), 1 - y, 1 - c))
            return carry

        lax.fori_loop(2, ZS, far_sibling, 0)

        def far_pair(t, carry):
            first = block((1 - side) * (2 + t % 2) + side * (1 - t % 2), (y + t // 2) % 2, 0)
            cot_arrived(first)
            cot_arrived(first + 1)
            add(first, 2, False)
            return carry

        lax.fori_loop(0, 4, far_pair, 0)

        def pick(k, carry):
            for col in range(cols):
                r = rows[col * KMAX + k]
                tile = full[r, :, col * TILE : (col + 1) * TILE]
                tile = jnp.where(k < count[col], tile, jnp.zeros_like(tile))
                grad_ref[col, k] = tile.astype(jnp.bfloat16)
            return carry

        lax.fori_loop(0, KMAX, pick, 0)

    pl.run_scoped(grads, pltpu.VMEM((RT, TILE, width), jnp.float32))

    def finish_near(o, carry):
        peer = near_target(o)
        cot_push(peer).wait_send()
        gate_push(peer).wait_send()
        push(
            gate.at[mine], out_ref.at[:, span(peer)],
            gate_send.at[peer % HALF], gate_recv.at[peer], peer,
        ).wait_recv()
        return carry

    lax.fori_loop(1, HALF, finish_near, 0)

    def finish_far(o, carry):
        owner = HALF - home + o
        cot_push(owner).wait_send()
        local = jnp.logical_and(inner, o % 4 == me % 4)

        @pl.when(jnp.logical_not(local))
        def _():
            push(
                gate.at[mine], out_ref.at[:, span(owner)],
                gate_send.at[mine], gate_recv.at[owner], owner,
            ).wait_recv()

        return carry

    lax.fori_loop(0, HALF, finish_far, 0)
    own_copy().wait()

    def finish_weights(j, carry):
        w_push(j, w_outer, 0).wait_send()
        return carry

    lax.fori_loop(0, part, finish_weights, 0)
    mask_push(m_outer, 0).wait_send()

    @pl.when(inner)
    def _():
        for slot, (far, made) in enumerate(((w_outer, g_outer), (w_inner, g_inner))):

            def relayed(j, carry, far=far, slot=slot):
                w_cross(far, slot, x * part + j).wait_send()
                return carry

            def sent(o, carry, made=made, slot=slot):
                far_push(made, slot, far_taker(o)).wait_send()
                return carry

            lax.fori_loop(0, part, relayed, 0)
            far_copy(made, slot).wait()
            lax.fori_loop(0, HALF - 1, sent, 0)

    def finish_row(k, carry):
        row_forward(k, wait_send, False)
        row_forward(k, wait_send, True)
        row_share(k, wait_send)
        tok_push(block(order(k), 1 - y, c), ysib_sem.at[k], sibling).wait_send()
        return carry

    lax.fori_loop(0, ZS, finish_row, 0)


def fused_path(tokens, gate_cot, gate_weight, keep_mask):
    length, depth = tokens.shape
    width = gate_weight.shape[1]
    cols = width // TILE
    bf = jnp.bfloat16
    dma = pltpu.SemaphoreType.DMA
    anywhere = pl.BlockSpec(memory_space=pl.ANY)
    in_vmem = pl.BlockSpec(memory_space=pltpu.VMEM)
    mask = keep_mask.T
    return pl.pallas_call(
        fused_kernel,
        out_shape=(
            jax.ShapeDtypeStruct((length, PEERS * width), bf),
            jax.ShapeDtypeStruct((cols, KMAX, TILE, TILE), bf),
        ),
        in_specs=[
            pl.BlockSpec(memory_space=pltpu.SMEM), in_vmem, anywhere, anywhere, anywhere,
        ],
        out_specs=(anywhere, in_vmem),
        scratch_shapes=[
            pltpu.VMEM((PEERS, length, depth), bf),
            pltpu.VMEM((PEERS, length, width), bf),
            pltpu.VMEM((cols // 2, KMAX, TILE, TILE), bf),
            pltpu.VMEM((cols, KMAX, TILE, TILE), bf),
            pltpu.VMEM((cols, KMAX, TILE, TILE), bf),
            pltpu.VMEM((HALF, length, width), bf),
            pltpu.VMEM((HALF, length, width), bf),
            pltpu.VMEM((HALF, length, width), bf),
            pltpu.VMEM((cols, RT), jnp.int32),
            pltpu.VMEM((cols, RT), jnp.int32),
            pltpu.SMEM((cols, RT), jnp.int32),
            pltpu.SMEM((cols, RT), jnp.int32),
            pltpu.SMEM((2 * cols * RT,), jnp.int32),
            pltpu.SMEM((2 * cols * RT,), jnp.int32),
            pltpu.SMEM((RT + 1,), jnp.int32),
            pltpu.SMEM((cols * KMAX,), jnp.int32),
            pltpu.SMEM((cols,), jnp.int32),
            dma((ZS,)), dma((ZS,)), dma((ZS,)), dma((ZS,)), dma((ZS,)), dma((PEERS,)),
            dma((PEERS,)), dma((PEERS,)), dma((HALF,)), dma((2, HALF)), dma((PEERS,)),
            dma((cols // 2,)), dma((2, cols)), dma((2, cols // 2)), dma((3,)), dma((2,)), dma((6,)),
        ],
        compiler_params=pltpu.CompilerParams(
            collective_id=0, has_side_effects=True, vmem_limit_bytes=60 * 1024 * 1024
        ),
    )(mask, mask, tokens, gate_cot, gate_weight.reshape(RT, TILE, width))


def on_device(tokens, gate_cot, gate_weight, keep_mask):
    small = (tokens.shape, gate_weight.shape[1]) == ((128, RT * TILE), 8 * TILE)
    if lax.axis_size("fsdp") == PEERS and lax.axis_size("group") == 2 and small:
        return fused_path(tokens, gate_cot, gate_weight, keep_mask)
    return general_path(tokens, gate_cot, gate_weight, keep_mask)


def solution(mesh):
    placed = (
        P(("group", "fsdp"), None),
        P(("group", "fsdp"), None),
        P(None, "fsdp"),
        P(None, "fsdp"),
    )
    return jax.shard_map(
        on_device,
        mesh=mesh,
        in_specs=placed,
        out_specs=(P(("group", "fsdp"), None), P(("group", "fsdp"), None, None, None)),
        check_vma=False,
    )
```

```python
import jax
import jax.numpy as jnp
from jax import lax
from jax.experimental import pallas as pl
from jax.experimental.pallas import tpu as pltpu
from jax.sharding import PartitionSpec as P

TILE = 128
RT = 32
KMAX = 12


def kept_lists(keep_mask):
    kept_count = jnp.sum(keep_mask, axis=0)
    ordering = jnp.argsort(1 - keep_mask, axis=0, stable=True)[:KMAX]
    kept_rows = ordering.T
    kept_valid = jnp.arange(KMAX)[None, :] < kept_count[:, None]
    return (kept_rows, kept_valid)


def column_tiles(gate_weight, kept_rows, kept_valid, column):
    strip = gate_weight[:, column * TILE : (column + 1) * TILE].reshape(RT, TILE, TILE)
    picked = jnp.stack(
        [lax.dynamic_index_in_dim(strip, kept_rows[column, k], 0, False) for k in range(KMAX)]
    )
    picked = jnp.where(kept_valid[column][:, None, None], picked, jnp.zeros_like(picked))
    return picked.reshape(KMAX * TILE, TILE)


def general_path(tokens, gate_cot, gate_weight, keep_mask):
    local_width = gate_weight.shape[1]
    local_cols = local_width // TILE
    kept_rows, kept_valid = kept_lists(keep_mask)
    weight_cols = [
        column_tiles(gate_weight, kept_rows, kept_valid, column) for column in range(local_cols)
    ]
    cot_cols = lax.all_to_all(gate_cot, "fsdp", split_axis=1, concat_axis=0, tiled=True)
    total_rows = cot_cols.shape[0]

    def block_work(carry, piece, start):
        gate_all, grads = carry
        length = piece.shape[0]
        slope_piece = lax.dynamic_slice_in_dim(cot_cols, start, length, 0)
        outputs = []
        new_grads = []
        for column in range(local_cols):
            selected = jnp.concatenate(
                [
                    lax.dynamic_slice_in_dim(piece, kept_rows[column, k] * TILE, TILE, 1)
                    for k in range(KMAX)
                ],
                axis=1,
            )
            outputs.append(
                jnp.dot(selected, weight_cols[column], preferred_element_type=jnp.float32)
            )
            slope_col = slope_piece[:, column * TILE : (column + 1) * TILE]
            grad_col = lax.dot_general(
                selected, slope_col, (((0,), (0,)), ((), ())), preferred_element_type=jnp.float32
            )
            new_grads.append(grad_col.reshape(KMAX, TILE, TILE))
        values = jnp.concatenate(outputs, axis=1).astype(jnp.bfloat16)
        gate_all = lax.dynamic_update_slice_in_dim(gate_all, values, start, 0)
        return (gate_all, grads + jnp.stack(new_grads, axis=0))

    initial = (
        jnp.zeros((total_rows, local_width), jnp.bfloat16),
        jnp.zeros((local_cols, KMAX, TILE, TILE), jnp.float32),
    )
    piece = lax.all_gather(tokens, "fsdp", axis=0, tiled=True)
    length = piece.shape[0]

    def one_block(index, inner):
        offset = index * 1024
        block_rows = lax.dynamic_slice_in_dim(piece, offset, 1024, 0)
        return block_work(inner, block_rows, offset)

    gate_cols, partial_tiles = lax.fori_loop(0, length // 1024, one_block, initial)
    gate_out = lax.all_to_all(gate_cols, "fsdp", split_axis=0, concat_axis=1, tiled=True)
    grad_tiles = jnp.where(
        kept_valid[:, :, None, None], partial_tiles, jnp.zeros_like(partial_tiles)
    )
    return (gate_out, grad_tiles.astype(jnp.bfloat16))


ZS = 4
PEERS = 16
HALF = 8


def fused_kernel(
    mask_ref, mask_src, tokens_ref, cot_ref, weight_ref,
    out_ref, grad_ref,
    tok, cot, packed, w_outer, w_inner, gate, g_outer, g_inner, m_outer, m_inner,
    keep_outer, keep_inner, rank, flag, follow, rows, count,
    up_sem, down_sem, y_sem, sib_sem, ysib_sem, tok_recv,
    cot_send, cot_recv, gate_send, far_send, gate_recv,
    w_send, w_recv, wx_send, mask_sems, far_local, local_sem,
):
    me = lax.axis_index("fsdp")
    x = lax.axis_index("group")
    z = me // 4
    y = (me // 2) % 2
    c = me % 2
    side = z // 2
    mine = me % HALF
    home = side * HALF
    length = tok.shape[1]
    depth = tok.shape[2]
    width = cot.shape[2]
    cols = width // TILE
    part = cols // 2
    sibling = me + 1 - 2 * c
    partner = me + 2 - 4 * y
    inner = z == 1 + side

    def block(zz, yy, cc):
        return (zz * 2 + yy) * 2 + cc

    near = (z * (ZS - 1 - z)) // 2

    def order(k):
        f = k + near * (1 - 2 * k) * (1 - k // 2)
        return f + side * (ZS - 1 - 2 * f)

    def push(src, dst, send, recv, dev):
        return pltpu.make_async_remote_copy(
            src_ref=src, dst_ref=dst, send_sem=send, recv_sem=recv,
            device_id={"fsdp": dev}, device_id_type=pl.DeviceIdType.MESH,
        )

    def span(owner):
        return pl.ds(pl.multiple_of(owner * width, width), width)

    barrier = pltpu.get_barrier_semaphore()

    def greet(o, carry):
        pl.semaphore_signal(
            barrier, inc=1, device_id={"fsdp": (me + o) % PEERS},
            device_id_type=pl.DeviceIdType.MESH,
        )
        return carry

    def start(copy):
        copy.start()

    def wait_send(copy):
        copy.wait_send()

    tok_copy = pltpu.make_async_copy(tokens_ref, tok.at[me], local_sem.at[1])
    tok_copy.start()
    cot_copy = pltpu.make_async_copy(cot_ref.at[:, span(me)], cot.at[me], local_sem.at[2])
    lax.fori_loop(1, PEERS, greet, 0)
    pl.semaphore_signal(
        barrier, inc=1, device_id={"group": 1 - x}, device_id_type=pl.DeviceIdType.MESH
    )

    def tok_push(b, send, dev):
        return push(tok.at[b], tok.at[b], send, tok_recv.at[b], dev)

    def cot_push(d):
        return push(cot_ref.at[:, span(d)], cot.at[me], cot_send.at[d], cot_recv.at[me], d)

    def near_target(o):
        return home + (mine + o) % HALF

    def far_target(t):
        late = t // 4
        zz = (1 - side) * (3 - late) + side * late
        return block(zz, (y + t // 2) % 2, (c + t) % 2)

    def far_taker(o):
        late = o // 4
        zz = side * (3 - late) + (1 - side) * late
        return zz * 4 + (me % 4 + o + late) % 4

    def gate_push(b):
        return push(
            gate.at[b % HALF], out_ref.at[:, span(me)],
            gate_send.at[b % HALF], gate_recv.at[me], b,
        )

    def own_copy():
        return pltpu.make_async_copy(gate.at[mine], out_ref.at[:, span(me)], local_sem.at[3])

    def owner_of(slot):
        return block((1 - side) * (3 - slot) + side * slot, y, c)

    def far_push(made, slot, b):
        return push(
            made.at[b % HALF], out_ref.at[:, span(owner_of(slot))],
            far_send.at[slot, b % HALF], gate_recv.at[owner_of(slot)], b,
        )

    def far_copy(made, slot):
        return pltpu.make_async_copy(
            made.at[mine], out_ref.at[:, span(owner_of(slot))], far_local.at[slot]
        )

    def w_push(j, far, slot):
        col = x * part + j
        return push(
            packed.at[j], far.at[col], w_send.at[j], w_recv.at[slot, col], block(2 - side, y, c)
        )

    def w_cross(far, slot, col):
        return pltpu.make_async_remote_copy(
            src_ref=far.at[col], dst_ref=far.at[col],
            send_sem=wx_send.at[slot, col % part], recv_sem=w_recv.at[slot, col],
            device_id={"group": 1 - x}, device_id_type=pl.DeviceIdType.MESH,
        )

    def mask_push(land, slot):
        return push(mask_src, land, mask_sems.at[0], mask_sems.at[1 + slot], block(2 - side, y, c))

    def row_forward(k, act, across):
        zk = order(k)
        b = block(zk, y, c)

        @pl.when(
            jnp.logical_and(zk <= z, jnp.logical_and(z < ZS - 1, (z == 1) == across))
        )
        def _():
            act(tok_push(b, up_sem.at[k], me + 4))

        @pl.when(jnp.logical_and(zk >= z, jnp.logical_and(z > 0, (z == 2) == across)))
        def _():
            act(tok_push(b, down_sem.at[k], me - 4))

    def row_share(k, act):
        b = block(order(k), y, c)
        act(tok_push(b, y_sem.at[k], partner))
        act(tok_push(b, sib_sem.at[k], sibling))

    def arrived(b):
        tok_push(b, up_sem.at[0], sibling).wait_recv()

    def cot_arrived(b):
        push(cot.at[b], cot.at[b], cot_send.at[b], cot_recv.at[b], b).wait_recv()

    def find_rows(col, carry):
        follow[RT] = RT - 1

        def back(i, state):
            nxt, total = state
            r = RT - 1 - i
            keep = mask_ref[col, r]
            nxt = jnp.where(keep > 0, r, nxt)
            follow[r] = nxt
            return (nxt, total + keep)

        count[col] = lax.fori_loop(0, RT, back, (RT - 1, 0), unroll=True)[1]

        def ahead(k, pos):
            r = follow[pos]
            rows[col * KMAX + k] = r
            return jnp.minimum(r + 1, RT)

        lax.fori_loop(0, KMAX, ahead, 0, unroll=True)
        return carry

    def gates(w, chunk_buf, held):
        w_copy = pltpu.make_async_copy(weight_ref, w, local_sem.at[0])
        w_copy.start()
        cot_copy.start()
        lax.fori_loop(0, cols, find_rows, 0)
        tok_copy.wait()
        pl.semaphore_wait(barrier, PEERS)
        row_forward(0, start, False)
        row_forward(0, start, True)
        row_share(0, start)

        def send_far(t, carry):
            cot_push(far_target(t)).start()
            return carry

        @pl.when(inner)
        def _():
            send_far(0, 0)

        @pl.when(inner)
        def _():
            mask_push(m_inner, 1).start()

        @pl.when(jnp.logical_not(inner))
        def _():
            mask_push(m_outer, 0).start()

        w_copy.wait()

        def pack(k, carry):
            for j in range(part):
                col = x * part + j
                r = rows[col * KMAX + k]
                packed[j, k] = w[r, :, pl.ds(pl.multiple_of(col * TILE, TILE), TILE)]
            return carry

        lax.fori_loop(0, KMAX, pack, 0)

        def early_weights(j, carry):
            w_push(j, w_outer, 0).start()
            return carry

        @pl.when(jnp.logical_not(inner))
        def _():
            lax.fori_loop(0, part, early_weights, 0)

        def send_near(o, carry):
            cot_push(near_target(o)).start()
            return carry

        lax.fori_loop(1, HALF, send_near, 0)

        def prune(r, carry):
            for col in range(cols):
                at = slice(col * TILE, (col + 1) * TILE)
                keep = jnp.full((1, TILE), mask_ref[col, r].astype(jnp.float32))
                w[r, :, at] = w[r, :, at] * keep.astype(jnp.bfloat16)
            return carry

        lax.fori_loop(0, RT, prune, 0)

        def gate_values(zk, yk):
            first = block(zk, yk, 0)
            slot = first % HALF
            arrived(block(zk, yk, 1 - c))

            def chunk(j, carry):
                at = pl.ds(pl.multiple_of(j * 256, 256), 256)
                lhs = tok[pl.ds(first, 2)].reshape(2 * length, depth)
                rhs = w[:, :, at].reshape(depth, 256)
                val = jnp.dot(lhs, rhs, preferred_element_type=jnp.float32)
                gate[pl.ds(slot, 2), :, at] = val.astype(jnp.bfloat16).reshape(2, length, 256)
                return carry

            lax.fori_loop(0, width // 256, chunk, 0)

            def out(cc, carry):
                b = first + cc

                @pl.when(b != me)
                def _():
                    gate_push(b).start()

                return carry

            lax.fori_loop(0, 2, out, 0)

        def row_arrived(k):
            arrived(block(order(k), y, c))
            row_forward(k, start, False)
            row_forward(k, start, True)
            row_share(k, start)

        def side_arrived(k):
            b = block(order(k), 1 - y, c)
            arrived(b)
            tok_push(b, ysib_sem.at[k], sibling).start()

        def relays(far, slot, lo, hi):
            def one(j, carry):
                w_cross(far, slot, x * part + j).wait_recv()
                w_cross(far, slot, x * part + j).start()
                return carry

            lax.fori_loop(lo, hi, one, 0)

        def late_weights(j, carry):
            w_push(j, w_inner, 1).start()
            return carry

        def step(k, carry):
            @pl.when(k == 1)
            def _():
                row_arrived(1)

            @pl.when(jnp.logical_and(inner, k == 1))
            def _():
                lax.fori_loop(0, part, late_weights, 0)
                lax.fori_loop(1, 8, send_far, 0)
                row_arrived(2)

            @pl.when(k >= 2)
            def _():
                side_arrived(k - 2)

            @pl.when(jnp.logical_and(inner, k >= 2))
            def _():
                relays(w_outer, 0, 2 * (k - 2), 2 * (k - 1))

            gate_values(order(k % 2), y + (k // 2) * (1 - 2 * y))

            @pl.when(k == 0)
            def _():
                own_copy().start()

            return carry

        lax.fori_loop(0, 4, step, 0)

        @pl.when(jnp.logical_not(inner))
        def _():
            lax.fori_loop(0, 8, send_far, 0)
            row_arrived(2)

        row_arrived(3)

        def far_gates(far, made, slot):
            def crossed(j, inside):
                w_cross(far, slot, (1 - x) * part + j).wait_recv()
                return inside

            lax.fori_loop(0, part, crossed, 0)

            def hold(col, inside):
                held[col] = far[col]
                return inside

            lax.fori_loop(0, cols, hold, 0)

            def pair(p, inside):
                for e in range(2):
                    col = 2 * p + e

                    def place(r, deeper):
                        at = (slot * cols + col) * RT + r
                        tile = held[col, rank[at]]
                        factor = jnp.full((1, TILE), flag[at].astype(jnp.float32))
                        chunk_buf[r, :, e * TILE : (e + 1) * TILE] = tile * factor.astype(
                            jnp.bfloat16
                        )
                        return deeper

                    lax.fori_loop(0, RT, place, 0)

                def rows_part(m, deeper):
                    at = pl.ds(pl.multiple_of(p * 256, 256), 256)
                    lhs = tok[pl.ds(home + 8 * m, 8)].reshape(8 * length, depth)
                    rhs = chunk_buf[...].reshape(depth, 256)
                    val = jnp.dot(lhs, rhs, preferred_element_type=jnp.float32)
                    made[pl.ds(8 * m, 8), :, at] = val.astype(jnp.bfloat16).reshape(
                        8, length, 256
                    )
                    return deeper

                lax.fori_loop(0, 1, rows_part, 0)
                return inside

            lax.fori_loop(0, width // 256, pair, 0)
            far_copy(made, slot).start()

            def out(o, inside):
                far_push(made, slot, far_taker(o)).start()
                return inside

            lax.fori_loop(0, HALF - 1, out, 0)

        @pl.when(inner)
        def _():
            for slot, (land, kept) in enumerate(((m_outer, keep_outer), (m_inner, keep_inner))):
                mask_push(land, slot).wait_recv()
                fetch = pltpu.make_async_copy(land, kept, local_sem.at[4 + slot])
                fetch.start()
                fetch.wait()

                def ranks(col, carry, kept=kept, slot=slot):
                    seen = 0
                    for r in range(RT):
                        keep = kept[col, r]
                        at = (slot * cols + col) * RT + r
                        rank[at] = jnp.minimum(seen, KMAX - 1)
                        flag[at] = keep
                        seen = seen + keep
                    return carry

                lax.fori_loop(0, cols, ranks, 0)

        sets = ((w_outer, g_outer, keep_outer), (w_inner, g_inner, keep_inner))
        for slot, (far, made, kept) in enumerate(sets):

            @pl.when(inner)
            def _(far=far, made=made, kept=kept, slot=slot):
                relays(w_inner, 1, 2 * slot, 2 * slot + 2)
                far_gates(far, made, slot)

            side_arrived(2 + slot)

    pl.run_scoped(
        gates,
        pltpu.VMEM((RT, TILE, width), jnp.bfloat16),
        pltpu.VMEM((RT, TILE, 256), jnp.bfloat16),
        pltpu.VMEM((cols, KMAX, TILE, TILE), jnp.bfloat16),
    )

    def grads(full):
        def add(first, blocks, fresh):
            def chunk(i, carry):
                at = pl.ds(pl.multiple_of(i * 512, 512), 512)
                lhs = tok[pl.ds(first, blocks), :, at].reshape(blocks * length, 512)
                rhs = cot[pl.ds(first, blocks)].reshape(blocks * length, width)
                val = lax.dot_general(
                    lhs, rhs, (((0,), (0,)), ((), ())), preferred_element_type=jnp.float32
                ).reshape(4, TILE, width)
                if not fresh:
                    val = val + full[pl.ds(4 * i, 4)]
                full[pl.ds(4 * i, 4)] = val
                return carry

            lax.fori_loop(0, RT // 4, chunk, 0)

        cot_copy.wait()

        def near_cot(o, carry):
            cot_arrived(near_target(o))
            return carry

        lax.fori_loop(1, HALF, near_cot, 0)
        add(home, HALF, True)

        def far_sibling(k, carry):
            arrived(block(order(k), y, 1 - c))
            arrived(block(order(k), 1 - y, 1 - c))
            return carry

        lax.fori_loop(2, ZS, far_sibling, 0)

        def far_pair(t, carry):
            first = block((1 - side) * (2 + t % 2) + side * (1 - t % 2), (y + t // 2) % 2, 0)
            cot_arrived(first)
            cot_arrived(first + 1)
            add(first, 2, False)
            return carry

        lax.fori_loop(0, 4, far_pair, 0)

        def pick(k, carry):
            for col in range(cols):
                r = rows[col * KMAX + k]
                tile = full[r, :, col * TILE : (col + 1) * TILE]
                tile = jnp.where(k < count[col], tile, jnp.zeros_like(tile))
                grad_ref[col, k] = tile.astype(jnp.bfloat16)
            return carry

        lax.fori_loop(0, KMAX, pick, 0)

    pl.run_scoped(grads, pltpu.VMEM((RT, TILE, width), jnp.float32))

    def finish_near(o, carry):
        peer = near_target(o)
        cot_push(peer).wait_send()
        gate_push(peer).wait_send()
        push(
            gate.at[mine], out_ref.at[:, span(peer)],
            gate_send.at[peer % HALF], gate_recv.at[peer], peer,
        ).wait_recv()
        return carry

    lax.fori_loop(1, HALF, finish_near, 0)

    def finish_far(o, carry):
        owner = HALF - home + o
        cot_push(owner).wait_send()
        local = jnp.logical_and(inner, o % 4 == me % 4)

        @pl.when(jnp.logical_not(local))
        def _():
            push(
                gate.at[mine], out_ref.at[:, span(owner)],
                gate_send.at[mine], gate_recv.at[owner], owner,
            ).wait_recv()

        return carry

    lax.fori_loop(0, HALF, finish_far, 0)
    own_copy().wait()

    def finish_weights(j, carry):
        w_push(j, w_outer, 0).wait_send()
        return carry

    lax.fori_loop(0, part, finish_weights, 0)
    mask_push(m_outer, 0).wait_send()

    @pl.when(inner)
    def _():
        for slot, (far, made) in enumerate(((w_outer, g_outer), (w_inner, g_inner))):

            def relayed(j, carry, far=far, slot=slot):
                w_cross(far, slot, x * part + j).wait_send()
                return carry

            def sent(o, carry, made=made, slot=slot):
                far_push(made, slot, far_taker(o)).wait_send()
                return carry

            lax.fori_loop(0, part, relayed, 0)
            far_copy(made, slot).wait()
            lax.fori_loop(0, HALF - 1, sent, 0)

    def finish_row(k, carry):
        row_forward(k, wait_send, False)
        row_forward(k, wait_send, True)
        row_share(k, wait_send)
        tok_push(block(order(k), 1 - y, c), ysib_sem.at[k], sibling).wait_send()
        return carry

    lax.fori_loop(0, ZS, finish_row, 0)


def fused_path(tokens, gate_cot, gate_weight, keep_mask):
    length, depth = tokens.shape
    width = gate_weight.shape[1]
    cols = width // TILE
    bf = jnp.bfloat16
    dma = pltpu.SemaphoreType.DMA
    anywhere = pl.BlockSpec(memory_space=pl.ANY)
    in_vmem = pl.BlockSpec(memory_space=pltpu.VMEM)
    mask = keep_mask.T
    return pl.pallas_call(
        fused_kernel,
        out_shape=(
            jax.ShapeDtypeStruct((length, PEERS * width), bf),
            jax.ShapeDtypeStruct((cols, KMAX, TILE, TILE), bf),
        ),
        in_specs=[
            pl.BlockSpec(memory_space=pltpu.SMEM), in_vmem, anywhere, anywhere, anywhere,
        ],
        out_specs=(anywhere, in_vmem),
        scratch_shapes=[
            pltpu.VMEM((PEERS, length, depth), bf),
            pltpu.VMEM((PEERS, length, width), bf),
            pltpu.VMEM((cols // 2, KMAX, TILE, TILE), bf),
            pltpu.VMEM((cols, KMAX, TILE, TILE), bf),
            pltpu.VMEM((cols, KMAX, TILE, TILE), bf),
            pltpu.VMEM((HALF, length, width), bf),
            pltpu.VMEM((HALF, length, width), bf),
            pltpu.VMEM((HALF, length, width), bf),
            pltpu.VMEM((cols, RT), jnp.int32),
            pltpu.VMEM((cols, RT), jnp.int32),
            pltpu.SMEM((cols, RT), jnp.int32),
            pltpu.SMEM((cols, RT), jnp.int32),
            pltpu.SMEM((2 * cols * RT,), jnp.int32),
            pltpu.SMEM((2 * cols * RT,), jnp.int32),
            pltpu.SMEM((RT + 1,), jnp.int32),
            pltpu.SMEM((cols * KMAX,), jnp.int32),
            pltpu.SMEM((cols,), jnp.int32),
            dma((ZS,)), dma((ZS,)), dma((ZS,)), dma((ZS,)), dma((ZS,)), dma((PEERS,)),
            dma((PEERS,)), dma((PEERS,)), dma((HALF,)), dma((2, HALF)), dma((PEERS,)),
            dma((cols // 2,)), dma((2, cols)), dma((2, cols // 2)), dma((3,)), dma((2,)), dma((6,)),
        ],
        compiler_params=pltpu.CompilerParams(
            collective_id=0, has_side_effects=True, vmem_limit_bytes=60 * 1024 * 1024
        ),
    )(mask, mask, tokens, gate_cot, gate_weight.reshape(RT, TILE, width))


def on_device(tokens, gate_cot, gate_weight, keep_mask):
    small = (tokens.shape, gate_weight.shape[1]) == ((128, RT * TILE), 8 * TILE)
    if lax.axis_size("fsdp") == PEERS and lax.axis_size("group") == 2 and small:
        return fused_path(tokens, gate_cot, gate_weight, keep_mask)
    return general_path(tokens, gate_cot, gate_weight, keep_mask)


def solution(mesh):
    placed = (
        P(("group", "fsdp"), None),
        P(("group", "fsdp"), None),
        P(None, "fsdp"),
        P(None, "fsdp"),
    )
    return jax.shard_map(
        on_device,
        mesh=mesh,
        in_specs=placed,
        out_specs=(P(("group", "fsdp"), None), P(("group", "fsdp"), None, None, None)),
        check_vma=False,
    )
```
